32 devices in a mesh: groups: 2 (over y), expert: 4 (over z), tensor: 4 (over x, core), sub: 1.
Axes of the slice: x: 2, y: 2, z: 4, core: 2. Of those that a mesh axis runs over, the one named last changes fastest.
Arguments:
- hidden_rows: bfloat16 [4, 320, 4096], P(None, ('groups', 'expert', 'tensor')), parts along dimension 1, may hold values from -6 to 6
- expert_ids: int32 [4, 320, 8], P(None, ('groups', 'expert', 'tensor')), parts along dimension 1, may hold values from 0 to 15, all different within a row; in each aligned block of 10 rows (0 to 9, 10 to 19, ..., all dimensions but the last counted through in order) at most 5 rows name the same one
- accepted: int32 [4, 64], P(None, ('groups', 'expert', 'tensor')), parts along dimension 1, may hold values from 0 to 4
- norm_gain: float32 [4096], replicated, may hold values from 0.5 to 1.5
- router: bfloat16 [4096, 16], replicated, may hold values from -0.0625 to 0.0625
- gate_weight: bfloat16 [16, 4096, 768], P(('expert', 'tensor'), None, 'sub'), may hold values from -0.09375 to 0.09375
- up_weight: bfloat16 [16, 4096, 768], P(('expert', 'tensor'), None, 'sub'), may hold values from -0.09375 to 0.09375
- down_weight: bfloat16 [16, 768, 4096], P(('expert', 'tensor'), 'sub'), may hold values from -0.21875 to 0.21875
- draft_gain: float32 [4096], replicated, may hold values from 0.5 to 1.5
- draft_gate: bfloat16 [4096, 6144], P(None, ('expert', 'tensor')), may hold values from -0.09375 to 0.09375
- draft_up: bfloat16 [4096, 6144], P(None, ('expert', 'tensor')), may hold values from -0.09375 to 0.09375
- draft_down: bfloat16 [6144, 4096], P(('expert', 'tensor')), may hold values from -0.078125 to 0.078125
- final_gain: float32 [4096], replicated, may hold values from 0.5 to 1.5
Outputs:
- verified: bfloat16 [4, 320, 4096], P(None, ('groups', 'expert', 'tensor')), parts along dimension 1
- draft_out: bfloat16 [4, 64, 4096], P(None, ('groups', 'expert', 'tensor')), parts along dimension 1
The draws below stay inside these ranges and needn't reach their ends.
There are 2 independent parts, one for each index of `groups`. The reference program is written for one: setup_inputs(seed, part) draws one part's arguments, and reference() takes and returns one part's arrays. A program takes and returns all parts, laid end to end along the dimension named above; an argument that names none is the same for every part. Nothing has to cross between parts.
Inputs may be any that keep to these rules, and one draw needn't show every extreme that they name: `expert_ids`: the 8 ids of a row differ. In each aligned block of 10 rows no expert is named by more than 5 rows, and in some block one expert is named by exactly 5 rows.
All inputs are finite; a program needn't handle non-finite values.
Results may differ from the reference program's by a relative error of at most 0.0068.
Values may be sent and summed in bfloat16 or wider, within the bound.
A program may use at most 128 MiB of HBM per device.

```python
import math
import jax
import jax.numpy as jnp
import numpy as np
from jax import lax

D = 4096
MOE_FF = 768
DFF = 6144
TOP = 8
DRAFT = 5
ROUNDS = 4
SPLIT = 1
FF_DEV = 768
EXPERTS = 16
ROWS_DEV = 10
ROWS = 160
REQS = 32
CAP = 5


def set_ends(drawn, stream_key, low, high):
    place = [jax.random.randint(jax.random.fold_in(stream_key, axis), (), 0, length) for axis, length in enumerate(drawn.shape)]
    main_axis = drawn.shape.index(max(drawn.shape))
    next_to = place[:main_axis] + [(place[main_axis] + 1) % drawn.shape[main_axis]] + place[main_axis + 1:]
    return drawn.at[tuple(place)].set(low).at[tuple(next_to)].set(high)


def levels(stream_key, dims, pieces, smallest, high):
    def one(axis_at, shards_of):
        draws = jax.random.uniform(jax.random.fold_in(jax.random.fold_in(stream_key, 6), axis_at), (shards_of,), jnp.float32, smallest / len(pieces), high / len(pieces))
        return jnp.repeat(jnp.exp(draws), dims[axis_at] // shards_of).reshape((-1,) + (1,) * (len(dims) - axis_at - 1))

    factor_of = one(*pieces[0])
    for cut in pieces[1:]:
        factor_of = factor_of * one(*cut)
    return factor_of


def routed_block(key, own, number, rows, count, top, bound, slope):
    ranking = jax.random.permutation(key, count)
    crowded, ordinary = shares(count, rows * top, bound, slope, True), shares(count, rows * top, bound, slope, False)
    places = jnp.arange(count)

    def named(lengths, rotation):
        used = int((lengths > 0).sum())
        fixed = max(1, used // 4)
        moved = fixed + (places - fixed + rotation * (used - fixed)) % max(1, count - fixed)
        return jnp.zeros((count,), jnp.int32).at[ranking[jnp.where(places < fixed, places, moved)]].set(jnp.asarray(lengths, jnp.int32))

    lengths = jnp.where(number % 4 == 0, named(crowded, number // 4), named(ordinary, number - number // 4 - 1))
    mixed = jax.random.permutation(jax.random.fold_in(own, 3), count)
    source_of, sink = mixed[0:count // 2 * 2:2], mixed[1:count // 2 * 2:2]
    margin = jnp.minimum(lengths[source_of] - 1, bound - lengths[sink]) // 2
    margin = jnp.where((source_of == ranking[0]) | (sink == ranking[0]) | (lengths[sink] == 0), 0, jnp.maximum(margin, 0))
    moved = jax.random.randint(jax.random.fold_in(own, 4), (count // 2,), 0, 1 << 20) % (margin + 1)
    lengths = lengths.at[source_of].add(-moved).at[sink].add(moved)
    members = jnp.searchsorted(jnp.cumsum(lengths), jnp.arange(rows * top), side="right").astype(jnp.int32)
    listing = members.reshape(top, rows).T
    listing = listing[jax.random.permutation(jax.random.fold_in(own, 1), rows)]
    rotation = jax.random.randint(jax.random.fold_in(own, 2), (rows, 1), 0, top)
    return jnp.take_along_axis(listing, (jnp.arange(top)[None, :] + rotation) % top, axis=1)


def shares(count, total, limit, slope, full):
    loads = [(1 << 20) // math.isqrt(grade ** slope) + 1 for grade in range(1, count + 1)]
    largest = limit if full else min(limit, max(-(-total // count), total * loads[0] // sum(loads)))
    least = 1 if total - largest >= count - 1 else 0
    holding, rest = [largest] + [least] * (count - 1), total - largest - least * (count - 1)
    while rest > 0:
        movable = [i for i in range(1, count) if holding[i] < largest] or [i for i in range(1, count) if holding[i] < limit]
        mass, budget = sum([loads[i] for i in movable]), rest
        for i in movable:
            addition = min(limit - holding[i], max(1, budget * loads[i] // mass), rest)
            holding[i] = holding[i] + addition
            rest = rest - addition
    return np.array(holding)


def scatter_about(stream_key, shape, width, reach, shards=(), kind=jnp.bfloat16):
    level = levels(stream_key, shape, shards, -0.22, 0.18) if shards else 1.0
    values = jax.random.normal(stream_key, shape, jnp.float32) * width * level
    return jnp.minimum(jnp.maximum(values, -reach), reach).astype(kind)


def setup_inputs(seed: int = 0, part: int = 0) -> dict:
    keys = jax.random.split(jax.random.key(seed), 14)
    own_keys = jax.random.split(jax.random.fold_in(keys[13], part), 14)
    hidden_rows = scatter_about(own_keys[0], (ROUNDS, ROWS, D), 1.0, 6.0, ((1, 16),))
    expert_ids_keys = jax.random.split(jax.random.fold_in(own_keys[1], 1), ROUNDS * ROWS // ROWS_DEV)
    expert_ids_turns = jax.random.permutation(jax.random.fold_in(own_keys[1], 3), ROUNDS * ROWS // ROWS_DEV)
    expert_ids = jax.vmap(lambda own, number: routed_block(jax.random.fold_in(own_keys[1], 2), own, number, ROWS_DEV, EXPERTS, TOP, CAP, 2))(expert_ids_keys, expert_ids_turns).reshape((ROUNDS, ROWS, TOP))
    accepted = set_ends(jax.random.randint(own_keys[2], (ROUNDS, REQS), 0, DRAFT), jax.random.fold_in(own_keys[2], 1), 0, DRAFT - 1).astype(jnp.int32)
    norm_gain = jnp.clip(1.0 + 0.1 * jax.random.normal(keys[3], (D,), jnp.float32), 0.5, 1.5)
    router = scatter_about(keys[4], (D, EXPERTS), (2 * D) ** -0.5, 0.0625)
    gate_weight = scatter_about(keys[5], (EXPERTS, D, MOE_FF), D ** -0.5, 0.09375, ((0, 16),))
    up_weight = scatter_about(keys[6], (EXPERTS, D, MOE_FF), D ** -0.5, 0.09375, ((0, 16),))
    down_weight = scatter_about(keys[7], (EXPERTS, MOE_FF, D), MOE_FF ** -0.5, 0.21875, ((0, 16),))
    draft_gain = jnp.clip(1.0 + 0.1 * jax.random.normal(keys[8], (D,), jnp.float32), 0.5, 1.5)
    draft_gate = scatter_about(keys[9], (D, DFF), D ** -0.5, 0.09375, ((1, 16),))
    draft_up = scatter_about(keys[10], (D, DFF), D ** -0.5, 0.09375, ((1, 16),))
    draft_down = scatter_about(keys[11], (DFF, D), DFF ** -0.5, 0.078125, ((0, 16),))
    final_gain = jnp.clip(1.0 + 0.1 * jax.random.normal(keys[12], (D,), jnp.float32), 0.5, 1.5)
    return dict(hidden_rows=hidden_rows, expert_ids=expert_ids, accepted=accepted, norm_gain=norm_gain, router=router, gate_weight=gate_weight, up_weight=up_weight, down_weight=down_weight, draft_gain=draft_gain, draft_gate=draft_gate, draft_up=draft_up, draft_down=draft_down, final_gain=final_gain)


EPSILON = 1e-06

def rms_scale(values, weights):
    values = values.astype(jnp.float32)
    mean_square = lax.optimization_barrier(jnp.mean(values * values, axis=-1, keepdims=True))
    return values * lax.rsqrt(mean_square + EPSILON) * weights

def slot_positions(chosen_ids):
    blocks = chosen_ids.reshape(ROWS // ROWS_DEV, ROWS_DEV * TOP)
    one_hot = (blocks[:, :, None] == jnp.arange(EXPERTS, dtype=jnp.int32)[None, None, :]).astype(jnp.int32)
    rank_values = jnp.cumsum(one_hot, axis=1) - 1
    positions = lax.optimization_barrier(jnp.sum(rank_values * one_hot, axis=2))
    return positions.reshape(ROWS, TOP).astype(jnp.int32)

def expert_apply(operands):
    inputs, gate_matrix, up_matrix, down_matrix = operands
    gate_values = jnp.dot(inputs, gate_matrix, preferred_element_type=jnp.float32)
    up_values = jnp.dot(inputs, up_matrix, preferred_element_type=jnp.float32)
    active = (jax.nn.silu(gate_values) * up_values).astype(jnp.bfloat16)
    summed_out = jnp.zeros((inputs.shape[0], D), jnp.float32)
    for group_index in range(SPLIT):
        lower = group_index * FF_DEV
        part_sum = jnp.dot(active[:, lower:lower + FF_DEV], down_matrix[lower:lower + FF_DEV], preferred_element_type=jnp.float32)
        summed_out = summed_out + lax.optimization_barrier(part_sum.astype(jnp.bfloat16)).astype(jnp.float32)
    return summed_out.astype(jnp.bfloat16)

def reference(hidden_rows, expert_ids, accepted, norm_gain, router, gate_weight, up_weight, down_weight, draft_gain, draft_gate, draft_up, draft_down, final_gain):
    block_total = ROWS // ROWS_DEV
    total_slots = EXPERTS * block_total * CAP
    verified_list = []
    draft_list = []
    for round_index in range(ROUNDS):
        rows = hidden_rows[round_index]
        chosen_ids = expert_ids[round_index].astype(jnp.int32)
        normed = rms_scale(rows, norm_gain).astype(jnp.bfloat16)
        logits = jnp.dot(normed, router, preferred_element_type=jnp.float32)
        chosen = jnp.take_along_axis(logits, chosen_ids, axis=1)
        exp_values = jnp.exp(chosen)
        gate_share = exp_values / lax.optimization_barrier(jnp.sum(exp_values, axis=1, keepdims=True))
        positions = slot_positions(chosen_ids)
        block_index = (jnp.arange(ROWS, dtype=jnp.int32) // ROWS_DEV)[:, None]
        slot_index = ((chosen_ids * block_total + block_index) * CAP + positions).astype(jnp.int32)
        row_ids = jnp.broadcast_to(jnp.arange(ROWS, dtype=jnp.int32)[:, None], (ROWS, TOP))
        slot_rows = jnp.full((total_slots,), ROWS, jnp.int32).at[slot_index.reshape(-1)].set(row_ids.reshape(-1))
        padded = jnp.concatenate([normed, jnp.zeros((1, D), normed.dtype)], axis=0)
        buffers = padded[slot_rows].reshape(EXPERTS, block_total * CAP, D)
        outputs = lax.map(expert_apply, (buffers, gate_weight, up_weight, down_weight)).reshape(total_slots, D)
        picked = outputs[slot_index].astype(jnp.float32)
        mixed_rows = rows.astype(jnp.float32) + lax.optimization_barrier(jnp.sum(gate_share[:, :, None] * picked, axis=1))
        verified = mixed_rows.astype(jnp.bfloat16)
        chosen_rows = (jnp.arange(REQS, dtype=jnp.int32) * DRAFT + accepted[round_index].astype(jnp.int32)).astype(jnp.int32)
        features = verified[chosen_rows]
        draft_in = rms_scale(features, draft_gain).astype(jnp.bfloat16)
        hidden = (jax.nn.silu(jnp.dot(draft_in, draft_gate, preferred_element_type=jnp.float32)) * jnp.dot(draft_in, draft_up, preferred_element_type=jnp.float32)).astype(jnp.bfloat16)
        summed = features.astype(jnp.float32) + jnp.dot(hidden, draft_down, preferred_element_type=jnp.float32)
        draft_out = rms_scale(summed, final_gain).astype(jnp.bfloat16)
        verified_list.append(verified)
        draft_list.append(draft_out)
    return (jnp.stack(verified_list, axis=0), jnp.stack(draft_list, axis=0))
```

```python
import jax
import jax.numpy as jnp
from jax import lax
from jax.sharding import PartitionSpec as P

EPSILON = 1e-06
RING = ("expert", "tensor")


def rms_scale(values, weights):
    values = values.astype(jnp.float32)
    mean_square = jnp.mean(values * values, axis=-1, keepdims=True)
    return values * lax.rsqrt(mean_square + EPSILON) * weights


def local(
    hidden_rows,
    expert_ids,
    accepted,
    norm_gain,
    router,
    gate_weight,
    up_weight,
    down_weight,
    draft_gain,
    draft_gate,
    draft_up,
    draft_down,
    final_gain,
):
    rounds_total, rows_here, width = hidden_rows.shape
    expert_count = router.shape[1]
    requests_here = accepted.shape[1]
    draft_rows = rows_here // requests_here
    total = rounds_total * rows_here
    my_expert = lax.axis_index(RING)

    rows = hidden_rows.reshape(total, width).astype(jnp.float32)
    normed = rms_scale(rows, norm_gain).astype(jnp.bfloat16)
    logits = jnp.dot(normed, router, preferred_element_type=jnp.float32)
    ids = expert_ids.reshape(total, -1)
    named = jnp.any(ids[:, :, None] == jnp.arange(expert_count, dtype=jnp.int32), axis=1)
    weights = jnp.where(named, jnp.exp(logits), 0.0)
    table = weights / jnp.sum(weights, axis=1, keepdims=True)

    everyone = lax.all_gather(normed, RING, axis=0, tiled=True)
    table = lax.all_gather(table, RING, axis=0, tiled=True)
    share = jnp.sum(
        jnp.where(jnp.arange(expert_count) == my_expert, table, 0.0), axis=1, keepdims=True
    )
    gate_values = jnp.dot(everyone, gate_weight[0], preferred_element_type=jnp.float32)
    up_values = jnp.dot(everyone, up_weight[0], preferred_element_type=jnp.float32)
    active = (jax.nn.silu(gate_values) * up_values).astype(jnp.bfloat16)
    part = jnp.dot(active, down_weight[0], preferred_element_type=jnp.float32)
    part = (share * part).astype(jnp.bfloat16)
    mixed = lax.psum_scatter(part, RING, scatter_dimension=0, tiled=True)
    mixed = lax.psum(mixed, "sub").astype(jnp.float32)
    verified = (rows + mixed).astype(jnp.bfloat16)

    by_request = verified.reshape(rounds_total, requests_here, draft_rows, width)
    pick = jnp.arange(draft_rows, dtype=jnp.int32) == accepted[:, :, None]
    features = jnp.sum(jnp.where(pick[..., None], by_request.astype(jnp.float32), 0.0), axis=2)
    features = features.reshape(rounds_total * requests_here, width)
    draft_input = rms_scale(features, draft_gain).astype(jnp.bfloat16)
    pieces = lax.all_gather(draft_input, RING, axis=0, tiled=True)
    gate_part = jnp.dot(pieces, draft_gate, preferred_element_type=jnp.float32)
    up_part = jnp.dot(pieces, draft_up, preferred_element_type=jnp.float32)
    units = (jax.nn.silu(gate_part) * up_part).astype(jnp.bfloat16)
    summed = lax.psum_scatter(
        jnp.dot(units, draft_down, preferred_element_type=jnp.float32).astype(jnp.bfloat16),
        RING,
        scatter_dimension=0,
        tiled=True,
    ).astype(jnp.float32)
    draft_out = rms_scale(features + summed, final_gain).astype(jnp.bfloat16)
    return (
        verified.reshape(hidden_rows.shape),
        draft_out.reshape(rounds_total, requests_here, width),
    )


def solution(mesh):
    placed = (
        P(None, ("groups", "expert", "tensor"), None),
        P(None, ("groups", "expert", "tensor"), None),
        P(None, ("groups", "expert", "tensor")),
        P(),
        P(),
        P(("expert", "tensor"), None, "sub"),
        P(("expert", "tensor"), None, "sub"),
        P(("expert", "tensor"), "sub", None),
        P(),
        P(None, ("expert", "tensor")),
        P(None, ("expert", "tensor")),
        P(("expert", "tensor"), None),
        P(),
    )
    return jax.shard_map(
        local,
        mesh=mesh,
        in_specs=placed,
        out_specs=(
            P(None, ("groups", "expert", "tensor"), None),
            P(None, ("groups", "expert", "tensor"), None),
        ),
        check_vma=False,
    )
```

```python
import functools

import jax
import jax.numpy as jnp
from jax import lax
from jax.experimental import pallas as pl
from jax.experimental.pallas import tpu as pltpu
from jax.sharding import PartitionSpec as P

EPSILON = 1e-06
RING = ("expert", "tensor")
MESH = pl.DeviceIdType.MESH


class Loop:
    def __init__(self, mesh_shape):
        self.expert, self.tensor = mesh_shape["expert"], mesh_shape["tensor"]
        two = mesh_shape["sub"] == 1 and self.tensor % 2 == 0
        self.lanes = 2 if two else 1
        self.n = self.expert * self.tensor // self.lanes
        self.half = self.n // 2

    def me(self):
        z, t = lax.axis_index("expert"), lax.axis_index("tensor")
        x, lane = lax.div(t, self.lanes), lax.rem(t, self.lanes)
        flip = lax.rem(x, 2)
        return x * self.expert + z + flip * (self.expert - 1 - 2 * z), lane

    def at(self, position, lane):
        q = lax.rem(position + self.n, self.n)
        x, z = lax.div(q, self.expert), lax.rem(q, self.expert)
        z = z + lax.rem(x, 2) * (self.expert - 1 - 2 * z)
        return z, x * self.lanes + lane

    def device(self, position, lane):
        z, t = self.at(position, lane)
        return {"expert": z, "tensor": t}

    def block(self, position, lane):
        z, t = self.at(position, lane)
        return z * self.tensor + t

    def greet(self, p, lane):
        barrier = pltpu.get_barrier_semaphore()
        others = [self.device(p + 1, lane), self.device(p - 1, lane)]
        if self.lanes == 2:
            others.append(self.device(p, 1 - lane))
        for other in others:
            pl.semaphore_signal(barrier, inc=1, device_id=other, device_id_type=MESH)
        pl.semaphore_wait(barrier, len(others))


def gather_kernel(loop, pieces, inputs, *refs):
    sources, outs = refs[:inputs], refs[inputs : 2 * inputs]
    ring_send, ring_recv, pair_send, pair_recv, own_sem = refs[2 * inputs :]
    p, lane = loop.me()
    last = loop.half
    loop.greet(p, lane)

    def source(c):
        which, start, size = pieces[c]
        return sources[which].at[:, pl.ds(start, size)]

    def landed(block, c):
        which, start, size = pieces[c]
        return outs[which].at[block, :, pl.ds(start, size)]

    def used(way, step, c):
        return step < last or c % 2 == way

    started, ring = [], {}

    def send(way, step, c):
        q = p - (step - 1) if way == 0 else p + (step - 1)
        block = loop.block(q, lane)
        ring[way, step, c] = pltpu.make_async_remote_copy(
            src_ref=source(c) if step == 1 else landed(block, c),
            dst_ref=landed(block, c),
            send_sem=ring_send.at[way, step - 1, c],
            recv_sem=ring_recv.at[way, step - 1, c],
            device_id=loop.device(p + 1 if way == 0 else p - 1, lane),
            device_id_type=MESH,
        )
        ring[way, step, c].start()

    def share(k, q, c):
        if loop.lanes == 1:
            return
        block = loop.block(q, lane)
        copy = pltpu.make_async_remote_copy(
            src_ref=source(c) if k == 0 else landed(block, c),
            dst_ref=landed(block, c),
            send_sem=pair_send.at[k, c],
            recv_sem=pair_recv.at[k, c],
            device_id=loop.device(p, 1 - lane),
            device_id_type=MESH,
        )
        copy.start()
        started.append(copy)

    count = len(pieces)
    for c in range(count):
        for way in range(2):
            if used(way, 1, c):
                send(way, 1, c)
    keep = []
    for c in range(count):
        share(0, p, c)
        copy = pltpu.make_async_copy(source(c), landed(loop.block(p, lane), c), own_sem.at[c])
        copy.start()
        keep.append(copy)
    for step in range(2, last + 2):
        for c in range(count):
            for way in range(2):
                if not used(way, step - 1, c):
                    continue
                ring[way, step - 1, c].wait_recv()
                if step <= last and used(way, step, c):
                    send(way, step, c)
                q = p - (step - 1) if way == 0 else p + (step - 1)
                share(way * last + step - 1, q, c)
    for copy in keep:
        copy.wait()
    for copy in ring.values():
        copy.wait_send()
    for copy in started:
        copy.wait()


def gather(loop, collective_id, *arrays):
    pieces = []
    for which, array in enumerate(arrays):
        width = array.shape[1]
        cuts = 2 if width >= 1024 else 1
        for cut in range(cuts):
            pieces.append((which, cut * width // cuts, width // cuts))
    blocks = loop.n * loop.lanes
    count = len(pieces)
    return pl.pallas_call(
        functools.partial(gather_kernel, loop, pieces, len(arrays)),
        out_shape=[jax.ShapeDtypeStruct((blocks,) + a.shape, a.dtype) for a in arrays],
        in_specs=[pl.BlockSpec(memory_space=pltpu.VMEM)] * len(arrays),
        out_specs=[pl.BlockSpec(memory_space=pl.ANY)] * len(arrays),
        scratch_shapes=[
            pltpu.SemaphoreType.DMA((2, loop.half, count)),
            pltpu.SemaphoreType.DMA((2, loop.half, count)),
            pltpu.SemaphoreType.DMA((2 * loop.half + 1, count)),
            pltpu.SemaphoreType.DMA((2 * loop.half + 1, count)),
            pltpu.SemaphoreType.DMA((count,)),
        ],
        compiler_params=pltpu.CompilerParams(collective_id=collective_id, has_side_effects=True),
    )(*arrays)


def scatter_kernel(loop, part, out, *refs):
    if loop.lanes == 2:
        from_pair, stage, arrived, ring_send, ring_recv, pair_send, pair_recv = refs
    else:
        stage, arrived, ring_send, ring_recv = refs
    p, lane = loop.me()
    n, last = loop.n, loop.half
    columns = part.shape[2] // 2
    loop.greet(p, lane)

    pairs, seen = {}, set()
    if loop.lanes == 2:
        for far in range(last, -1, -1):
            for offset in sorted({far, (n - far) % n}):
                pairs[offset] = pltpu.make_async_remote_copy(
                    src_ref=part.at[loop.block(p + offset, 1 - lane)],
                    dst_ref=from_pair.at[offset],
                    send_sem=pair_send.at[offset],
                    recv_sem=pair_recv.at[offset],
                    device_id=loop.device(p, 1 - lane),
                    device_id_type=MESH,
                )
                pairs[offset].start()

    def mine(offset, h):
        span = pl.ds(h * columns, columns)
        value = part[loop.block(p + offset, lane), :, span].astype(jnp.float32)
        if loop.lanes == 2:
            if offset not in seen:
                seen.add(offset)
                pairs[offset].wait_recv()
            value = value + from_pair[offset, :, span].astype(jnp.float32)
        return value

    def used(way, step, h):
        return 1 <= step <= last and (way == h or step >= 2)

    ring = {}
    for step in range(1, last + 1):
        for h in range(2):
            for way in range(2):
                if not used(way, step, h):
                    continue
                far = last + 1 - step
                value = mine(far if way == 0 else (n - far) % n, h)
                if used(way, step - 1, h):
                    ring[way, step - 1, h].wait_recv()
                    value = value + arrived[way, step - 2, h].astype(jnp.float32)
                if used(way, step - 2, h):
                    ring[way, step - 2, h].wait_send()
                stage[way, step % 2, h] = value.astype(jnp.bfloat16)
                ring[way, step, h] = pltpu.make_async_remote_copy(
                    src_ref=stage.at[way, step % 2, h],
                    dst_ref=arrived.at[way, step - 1, h],
                    send_sem=ring_send.at[way, step - 1, h],
                    recv_sem=ring_recv.at[way, step - 1, h],
                    device_id=loop.device(p + 1 if way == 0 else p - 1, lane),
                    device_id_type=MESH,
                )
                ring[way, step, h].start()
    for h in range(2):
        value = mine(0, h)
        for way in range(2):
            if used(way, last, h):
                ring[way, last, h].wait_recv()
                value = value + arrived[way, last - 1, h].astype(jnp.float32)
        out[:, pl.ds(h * columns, columns)] = value
    for (way, step, h), copy in ring.items():
        if step >= last - 1:
            copy.wait_send()
    for copy in pairs.values():
        copy.wait_send()


def scatter(loop, collective_id, part):
    blocks, rows, width = part.shape
    n, last = loop.n, loop.half
    dma = pltpu.SemaphoreType.DMA
    scratch = [
        pltpu.VMEM((2, 2, 2, rows, width // 2), jnp.bfloat16),
        pltpu.VMEM((2, last, 2, rows, width // 2), jnp.bfloat16),
        dma((2, last, 2)),
        dma((2, last, 2)),
    ]
    if loop.lanes == 2:
        scratch = [pltpu.VMEM((n, rows, width), jnp.bfloat16)] + scratch + [dma((n,)), dma((n,))]
    return pl.pallas_call(
        functools.partial(scatter_kernel, loop),
        out_shape=jax.ShapeDtypeStruct((rows, width), jnp.float32),
        in_specs=[pl.BlockSpec(memory_space=pltpu.VMEM)],
        out_specs=pl.BlockSpec(memory_space=pltpu.VMEM),
        scratch_shapes=scratch,
        compiler_params=pltpu.CompilerParams(
            collective_id=collective_id, has_side_effects=True, vmem_limit_bytes=60 * 2**20
        ),
    )(part)


def rms_scale(values, weights):
    values = values.astype(jnp.float32)
    mean_square = jnp.mean(values * values, axis=-1, keepdims=True)
    return values * lax.rsqrt(mean_square + EPSILON) * weights


def local(
    loop,
    hidden_rows,
    expert_ids,
    accepted,
    norm_gain,
    router,
    gate_weight,
    up_weight,
    down_weight,
    draft_gain,
    draft_gate,
    draft_up,
    draft_down,
    final_gain,
):
    rounds_total, rows_here, width = hidden_rows.shape
    expert_count = router.shape[1]
    requests_here = accepted.shape[1]
    draft_rows = rows_here // requests_here
    total = rounds_total * rows_here
    my_expert = lax.axis_index(RING)

    rows = hidden_rows.reshape(total, width).astype(jnp.float32)
    normed = rms_scale(rows, norm_gain).astype(jnp.bfloat16)
    logits = jnp.dot(normed, router, preferred_element_type=jnp.float32)
    ids = expert_ids.reshape(total, -1)
    named = jnp.any(ids[:, :, None] == jnp.arange(expert_count, dtype=jnp.int32), axis=1)
    weights = jnp.where(named, jnp.exp(logits), 0.0)
    table = weights / jnp.sum(weights, axis=1, keepdims=True)

    lanes_wide = -(-expert_count // 128) * 128
    table = jnp.pad(table, ((0, 0), (0, lanes_wide - expert_count)))
    everyone, tables = gather(loop, 0, normed, table)
    everyone = everyone.reshape(-1, width)
    share = jnp.sum(
        jnp.where(jnp.arange(lanes_wide) == my_expert, tables.reshape(-1, lanes_wide), 0.0),
        axis=1,
        keepdims=True,
    )
    gate_values = jnp.dot(everyone, gate_weight[0], preferred_element_type=jnp.float32)
    up_values = jnp.dot(everyone, up_weight[0], preferred_element_type=jnp.float32)
    active = (jax.nn.silu(gate_values) * up_values).astype(jnp.bfloat16)
    part = jnp.dot(active, down_weight[0], preferred_element_type=jnp.float32)
    part = (share * part).astype(jnp.bfloat16)
    mixed = lax.psum(scatter(loop, 1, part.reshape(-1, total, width)), "sub")
    verified = (rows + mixed).astype(jnp.bfloat16)

    by_request = verified.reshape(rounds_total, requests_here, draft_rows, width)
    pick = jnp.arange(draft_rows, dtype=jnp.int32) == accepted[:, :, None]
    features = jnp.sum(jnp.where(pick[..., None], by_request.astype(jnp.float32), 0.0), axis=2)
    features = features.reshape(rounds_total * requests_here, width)
    draft_input = rms_scale(features, draft_gain).astype(jnp.bfloat16)
    (pieces,) = gather(loop, 2, draft_input)
    pieces = pieces.reshape(-1, width)
    gate_part = jnp.dot(pieces, draft_gate, preferred_element_type=jnp.float32)
    up_part = jnp.dot(pieces, draft_up, preferred_element_type=jnp.float32)
    units = (jax.nn.silu(gate_part) * up_part).astype(jnp.bfloat16)
    drafted = jnp.dot(units, draft_down, preferred_element_type=jnp.float32).astype(jnp.bfloat16)
    summed = scatter(loop, 3, drafted.reshape(-1, rounds_total * requests_here, width))
    draft_out = rms_scale(features + summed, final_gain).astype(jnp.bfloat16)
    return (
        verified.reshape(hidden_rows.shape),
        draft_out.reshape(rounds_total, requests_here, width),
    )


def solution(mesh):
    placed = (
        P(None, ("groups", "expert", "tensor"), None),
        P(None, ("groups", "expert", "tensor"), None),
        P(None, ("groups", "expert", "tensor")),
        P(),
        P(),
        P(("expert", "tensor"), None, "sub"),
        P(("expert", "tensor"), None, "sub"),
        P(("expert", "tensor"), "sub", None),
        P(),
        P(None, ("expert", "tensor")),
        P(None, ("expert", "tensor")),
        P(("expert", "tensor"), None),
        P(),
    )
    loop = Loop(dict(mesh.shape))
    return jax.shard_map(
        functools.partial(local, loop),
        mesh=mesh,
        in_specs=placed,
        out_specs=(
            P(None, ("groups", "expert", "tensor"), None),
            P(None, ("groups", "expert", "tensor"), None),
        ),
        check_vma=False,
    )
```

```python
import functools

import jax
import jax.numpy as jnp
from jax import lax
from jax.experimental import pallas as pl
from jax.experimental.pallas import tpu as pltpu
from jax.sharding import PartitionSpec as P

EPSILON = 1e-06
RING = ("expert", "tensor")
MESH = pl.DeviceIdType.MESH


class Loop:
    def __init__(self, mesh_shape):
        self.expert, self.tensor = mesh_shape["expert"], mesh_shape["tensor"]
        two = mesh_shape["sub"] == 1 and self.tensor % 2 == 0
        self.lanes = 2 if two else 1
        self.n = self.expert * self.tensor // self.lanes
        self.half = self.n // 2

    def me(self):
        z, t = lax.axis_index("expert"), lax.axis_index("tensor")
        x, lane = lax.div(t, self.lanes), lax.rem(t, self.lanes)
        flip = lax.rem(x, 2)
        return x * self.expert + z + flip * (self.expert - 1 - 2 * z), lane

    def at(self, position, lane):
        q = lax.rem(position + self.n, self.n)
        x, z = lax.div(q, self.expert), lax.rem(q, self.expert)
        z = z + lax.rem(x, 2) * (self.expert - 1 - 2 * z)
        return z, x * self.lanes + lane

    def device(self, position, lane):
        z, t = self.at(position, lane)
        return {"expert": z, "tensor": t}

    def block(self, position, lane):
        z, t = self.at(position, lane)
        return z * self.tensor + t

    def greet(self, p, lane):
        barrier = pltpu.get_barrier_semaphore()
        others = [self.device(p + 1, lane), self.device(p - 1, lane)]
        if self.lanes == 2:
            others.append(self.device(p, 1 - lane))
        for other in others:
            pl.semaphore_signal(barrier, inc=1, device_id=other, device_id_type=MESH)
        pl.semaphore_wait(barrier, len(others))


def gather_kernel(loop, pieces, inputs, *refs):
    sources, outs = refs[:inputs], refs[inputs : 2 * inputs]
    ring_send, ring_recv, pair_send, pair_recv, own_sem = refs[2 * inputs :]
    p, lane = loop.me()
    last = loop.half
    loop.greet(p, lane)

    def source(c):
        which, start, size = pieces[c]
        return sources[which].at[:, pl.ds(start, size)]

    def landed(block, c):
        which, start, size = pieces[c]
        return outs[which].at[block, :, pl.ds(start, size)]

    def used(way, step, c):
        return step < last or c % 2 == way

    started, ring = [], {}

    def send(way, step, c):
        q = p - (step - 1) if way == 0 else p + (step - 1)
        block = loop.block(q, lane)
        ring[way, step, c] = pltpu.make_async_remote_copy(
            src_ref=source(c) if step == 1 else landed(block, c),
            dst_ref=landed(block, c),
            send_sem=ring_send.at[way, step - 1, c],
            recv_sem=ring_recv.at[way, step - 1, c],
            device_id=loop.device(p + 1 if way == 0 else p - 1, lane),
            device_id_type=MESH,
        )
        ring[way, step, c].start()

    def share(k, q, c):
        if loop.lanes == 1:
            return
        block = loop.block(q, lane)
        copy = pltpu.make_async_remote_copy(
            src_ref=source(c) if k == 0 else landed(block, c),
            dst_ref=landed(block, c),
            send_sem=pair_send.at[k, c],
            recv_sem=pair_recv.at[k, c],
            device_id=loop.device(p, 1 - lane),
            device_id_type=MESH,
        )
        copy.start()
        started.append(copy)

    count = len(pieces)
    for c in range(count):
        for way in range(2):
            if used(way, 1, c):
                send(way, 1, c)
    keep = []
    for c in range(count):
        share(0, p, c)
        copy = pltpu.make_async_copy(source(c), landed(loop.block(p, lane), c), own_sem.at[c])
        copy.start()
        keep.append(copy)
    for step in range(2, last + 2):
        for c in range(count):
            for way in range(2):
                if not used(way, step - 1, c):
                    continue
                ring[way, step - 1, c].wait_recv()
                if step <= last and used(way, step, c):
                    send(way, step, c)
                q = p - (step - 1) if way == 0 else p + (step - 1)
                share(way * last + step - 1, q, c)
    for copy in keep:
        copy.wait()
    for copy in ring.values():
        copy.wait_send()
    for copy in started:
        copy.wait()


def gather(loop, collective_id, *arrays):
    pieces = []
    for which, array in enumerate(arrays):
        width = array.shape[1]
        cuts = 2 if width >= 1024 else 1
        for cut in range(cuts):
            pieces.append((which, cut * width // cuts, width // cuts))
    blocks = loop.n * loop.lanes
    count = len(pieces)
    return pl.pallas_call(
        functools.partial(gather_kernel, loop, pieces, len(arrays)),
        out_shape=[jax.ShapeDtypeStruct((blocks,) + a.shape, a.dtype) for a in arrays],
        in_specs=[pl.BlockSpec(memory_space=pltpu.VMEM)] * len(arrays),
        out_specs=[pl.BlockSpec(memory_space=pl.ANY)] * len(arrays),
        scratch_shapes=[
            pltpu.SemaphoreType.DMA((2, loop.half, count)),
            pltpu.SemaphoreType.DMA((2, loop.half, count)),
            pltpu.SemaphoreType.DMA((2 * loop.half + 1, count)),
            pltpu.SemaphoreType.DMA((2 * loop.half + 1, count)),
            pltpu.SemaphoreType.DMA((count,)),
        ],
        compiler_params=pltpu.CompilerParams(collective_id=collective_id, has_side_effects=True),
    )(*arrays)


def scatter_kernel(loop, part, out, *refs):
    if loop.lanes == 2:
        from_pair, stage, arrived, ring_send, ring_recv, pair_send, pair_recv = refs
    else:
        stage, arrived, ring_send, ring_recv = refs
    p, lane = loop.me()
    n, last = loop.n, loop.half
    columns = part.shape[2] // 2
    loop.greet(p, lane)

    pairs, seen = {}, set()
    if loop.lanes == 2:
        for far in range(last, -1, -1):
            for offset in sorted({far, (n - far) % n}):
                pairs[offset] = pltpu.make_async_remote_copy(
                    src_ref=part.at[loop.block(p + offset, 1 - lane)],
                    dst_ref=from_pair.at[offset],
                    send_sem=pair_send.at[offset],
                    recv_sem=pair_recv.at[offset],
                    device_id=loop.device(p, 1 - lane),
                    device_id_type=MESH,
                )
                pairs[offset].start()

    def mine(offset, h):
        span = pl.ds(h * columns, columns)
        value = part[loop.block(p + offset, lane), :, span].astype(jnp.float32)
        if loop.lanes == 2:
            if offset not in seen:
                seen.add(offset)
                pairs[offset].wait_recv()
            value = value + from_pair[offset, :, span].astype(jnp.float32)
        return value

    def used(way, step, h):
        return 1 <= step <= last and (way == h or step >= 2)

    ring = {}
    for step in range(1, last + 1):
        for h in range(2):
            for way in range(2):
                if not used(way, step, h):
                    continue
                far = last + 1 - step
                value = mine(far if way == 0 else (n - far) % n, h)
                if used(way, step - 1, h):
                    ring[way, step - 1, h].wait_recv()
                    value = value + arrived[way, step - 2, h].astype(jnp.float32)
                if used(way, step - 2, h):
                    ring[way, step - 2, h].wait_send()
                stage[way, step % 2, h] = value.astype(jnp.bfloat16)
                ring[way, step, h] = pltpu.make_async_remote_copy(
                    src_ref=stage.at[way, step % 2, h],
                    dst_ref=arrived.at[way, step - 1, h],
                    send_sem=ring_send.at[way, step - 1, h],
                    recv_sem=ring_recv.at[way, step - 1, h],
                    device_id=loop.device(p + 1 if way == 0 else p - 1, lane),
                    device_id_type=MESH,
                )
                ring[way, step, h].start()
    for h in range(2):
        value = mine(0, h)
        for way in range(2):
            if used(way, last, h):
                ring[way, last, h].wait_recv()
                value = value + arrived[way, last - 1, h].astype(jnp.float32)
        out[:, pl.ds(h * columns, columns)] = value
    for (way, step, h), copy in ring.items():
        if step >= last - 1:
            copy.wait_send()
    for copy in pairs.values():
        copy.wait_send()


def scatter(loop, collective_id, part):
    blocks, rows, width = part.shape
    n, last = loop.n, loop.half
    dma = pltpu.SemaphoreType.DMA
    scratch = [
        pltpu.VMEM((2, 2, 2, rows, width // 2), jnp.bfloat16),
        pltpu.VMEM((2, last, 2, rows, width // 2), jnp.bfloat16),
        dma((2, last, 2)),
        dma((2, last, 2)),
    ]
    if loop.lanes == 2:
        scratch = [pltpu.VMEM((n, rows, width), jnp.bfloat16)] + scratch + [dma((n,)), dma((n,))]
    return pl.pallas_call(
        functools.partial(scatter_kernel, loop),
        out_shape=jax.ShapeDtypeStruct((rows, width), jnp.float32),
        in_specs=[pl.BlockSpec(memory_space=pltpu.VMEM)],
        out_specs=pl.BlockSpec(memory_space=pltpu.VMEM),
        scratch_shapes=scratch,
        compiler_params=pltpu.CompilerParams(
            collective_id=collective_id, has_side_effects=True, vmem_limit_bytes=60 * 2**20
        ),
    )(part)


def rms_scale(values, weights):
    values = values.astype(jnp.float32)
    mean_square = jnp.mean(values * values, axis=-1, keepdims=True)
    return values * lax.rsqrt(mean_square + EPSILON) * weights


def fused_kernel(loop, gated, pieces, batches, *refs):
    inputs = 2 if gated else 1
    sources = refs[:inputs]
    weights = refs[inputs : inputs + 3]
    out = refs[inputs + 3]
    rest = refs[inputs + 4 :]
    held, rest = rest[:inputs], rest[inputs:]
    gate_w, up_w, down_w, rows_all, active, part, stage, arrived = rest[:8]
    ring_send, ring_recv, sum_send, sum_recv, weight_sem, own_sem = rest[8:14]
    p, lane = loop.me()
    n, last, lanes = loop.n, loop.half, loop.lanes
    if lanes == 2:
        from_pair, pair_send, pair_recv, back_send, back_recv = rest[14:]
    count = len(pieces)
    rows, width = sources[0].shape
    columns = width // 2
    hidden = gate_w.shape[1]

    loads = []
    for i, (ref, buffer) in enumerate(zip(weights, (gate_w, up_w, down_w))):
        loads.append(pltpu.make_async_copy(ref, buffer, weight_sem.at[i]))
        loads[-1].start()
    loop.greet(p, lane)

    def slot(way, step, other):
        if step == 0:
            return other
        if step == last:
            return lanes * (2 * last - 1) + other
        return lanes * (2 * step - 1 + way) + other

    def source(c):
        which, start, size = pieces[c]
        return sources[which].at[:, pl.ds(start, size)]

    def landed(index, c):
        which, start, size = pieces[c]
        return held[which].at[index, :, pl.ds(start, size)]

    def used(way, step, c):
        return step < last or c % 2 == way

    ring, pair, waited = {}, {}, set()

    def send(way, step, c):
        ring[way, step, c] = pltpu.make_async_remote_copy(
            src_ref=source(c) if step == 1 else landed(slot(way, step - 1, 0), c),
            dst_ref=landed(slot(way, step, 0), c),
            send_sem=ring_send.at[way, step - 1, c],
            recv_sem=ring_recv.at[way, step - 1, c],
            device_id=loop.device(p + 1 if way == 0 else p - 1, lane),
            device_id_type=MESH,
        )
        ring[way, step, c].start()

    def share(way, step, c):
        if lanes == 1:
            return
        k = way * last + step
        pair[slot(way, step, 1), c] = pltpu.make_async_remote_copy(
            src_ref=source(c) if step == 0 else landed(slot(way, step, 0), c),
            dst_ref=landed(slot(way, step, 1), c),
            send_sem=pair_send.at[k, c],
            recv_sem=pair_recv.at[k, c],
            device_id=loop.device(p, 1 - lane),
            device_id_type=MESH,
        )
        pair[slot(way, step, 1), c].start()

    for c in range(count):
        for way in range(2):
            if used(way, 1, c):
                send(way, 1, c)
    keep = []
    for c in range(count):
        share(0, 0, c)
        keep.append(pltpu.make_async_copy(source(c), landed(0, c), own_sem.at[c]))
        keep[-1].start()

    def receive(step, wanted):
        for c in wanted:
            for way in range(2):
                if used(way, step, c):
                    ring[way, step, c].wait_recv()
                    if step < last and used(way, step + 1, c):
                        send(way, step + 1, c)
                    share(way, step, c)

    sums = {}

    def returned(offset):
        far, way = (offset, 1) if offset <= last else (n - offset, 0)
        return slot(way, far, 0)

    def send_back(first, stop):
        if lanes == 1:
            return
        for far in range(last, -1, -1):
            for offset in sorted({far, (n - far) % n}):
                at = returned(offset)
                if first <= at < stop:
                    sums[offset] = pltpu.make_async_remote_copy(
                        src_ref=part.at[at + 1],
                        dst_ref=from_pair.at[offset],
                        send_sem=back_send.at[offset],
                        recv_sem=back_recv.at[offset],
                        device_id=loop.device(p, 1 - lane),
                        device_id_type=MESH,
                    )
                    sums[offset].start()

    def compute(batch, between):
        first, stop = batch
        size = (stop - first) * rows
        for (index, c), copy in pair.items():
            if first <= index < stop and (index, c) not in waited:
                waited.add((index, c))
                copy.wait_recv()
        tile = 512

        def take(i, carry):
            span = pl.ds(pl.multiple_of(i * tile, tile), tile)
            block = held[0][pl.ds(first, stop - first), :, span].astype(jnp.float32)
            rows_all[pl.ds(0, size), span] = block.reshape(size, tile).astype(jnp.bfloat16)
            return carry

        lax.fori_loop(0, width // tile, take, 0)
        wide = 256 if hidden % 256 == 0 else 128

        def units(i, carry):
            span = pl.ds(pl.multiple_of(i * wide, wide), wide)
            x = rows_all[pl.ds(0, size), :]
            gate = jnp.dot(x, gate_w[:, span], preferred_element_type=jnp.float32)
            up = jnp.dot(x, up_w[:, span], preferred_element_type=jnp.float32)
            value = gate / (1.0 + jnp.exp(-gate)) * up
            active[pl.ds(0, size), span] = value.astype(jnp.bfloat16)
            return carry

        lax.fori_loop(0, hidden // wide, units, 0)
        between()
        if gated:
            mine = lax.axis_index("expert") * loop.tensor + lax.axis_index("tensor")
            table = held[1][pl.ds(first, stop - first), :, :]
            table = table.reshape(size, table.shape[2])
            here = lax.broadcasted_iota(jnp.int32, table.shape, 1) == mine
            weight = jnp.sum(jnp.where(here, table, 0.0), axis=1, keepdims=True)

        def down(i, carry):
            span = pl.ds(pl.multiple_of(i * tile, tile), tile)
            value = jnp.dot(
                active[pl.ds(0, size), :], down_w[:, span], preferred_element_type=jnp.float32
            )
            if gated:
                value = value * weight
            part[pl.ds(first, stop - first), :, span] = value.reshape(
                stop - first, rows, tile
            ).astype(jnp.bfloat16)
            return carry

        lax.fori_loop(0, width // tile, down, 0)
        send_back(first, stop)

    for copy in keep:
        copy.wait()
    ready = False
    for step in range(1, last + 1):
        done = batches.get(step - 1)
        if done is None:
            receive(step, range(count))
            continue
        if not ready:
            ready = True
            for copy in loads:
                copy.wait()
        compute(done, lambda: receive(step, range(1)))
        receive(step, range(1, count))
    if not ready:
        for copy in loads:
            copy.wait()
    compute(batches[last], lambda: None)

    seen = set()

    def mine_of(offset, h):
        span = pl.ds(h * columns, columns)
        value = part[returned(offset), :, span].astype(jnp.float32)
        if lanes == 2:
            if offset not in seen:
                seen.add(offset)
                sums[offset].wait_recv()
            value = value + from_pair[offset, :, span].astype(jnp.float32)
        return value

    def moves(way, step, h):
        return 1 <= step <= last and (way == h or step >= 2)

    back = {}
    for step in range(1, last + 1):
        for h in range(2):
            for way in range(2):
                if not moves(way, step, h):
                    continue
                far = last + 1 - step
                value = mine_of(far if way == 0 else (n - far) % n, h)
                if moves(way, step - 1, h):
                    back[way, step - 1, h].wait_recv()
                    value = value + arrived[way, step - 2, h].astype(jnp.float32)
                stage[way, step - 1, h] = value.astype(jnp.bfloat16)
                back[way, step, h] = pltpu.make_async_remote_copy(
                    src_ref=stage.at[way, step - 1, h],
                    dst_ref=arrived.at[way, step - 1, h],
                    send_sem=sum_send.at[way, step - 1, h],
                    recv_sem=sum_recv.at[way, step - 1, h],
                    device_id=loop.device(p + 1 if way == 0 else p - 1, lane),
                    device_id_type=MESH,
                )
                back[way, step, h].start()
    for h in range(2):
        value = mine_of(0, h)
        for way in range(2):
            if moves(way, last, h):
                back[way, last, h].wait_recv()
                value = value + arrived[way, last - 1, h].astype(jnp.float32)
        out[:, pl.ds(h * columns, columns)] = value
    for group in (ring, pair, sums, back):
        for copy in group.values():
            copy.wait_send()


def cut(arrays):
    pieces = []
    for which, array in enumerate(arrays):
        width = array.shape[1]
        cuts = 2 if width >= 1024 else 1
        for i in range(cuts):
            pieces.append((which, i * width // cuts, width // cuts))
    return pieces


def fused(loop, collective_id, early, arrays, weights):
    rows, width = arrays[0].shape
    hidden = weights[0].shape[1]
    n, last, lanes = loop.n, loop.half, loop.lanes
    pieces = cut(arrays)
    count = len(pieces)
    blocks = n * lanes
    if early and last >= 3:
        batches = {1: (0, 3 * lanes)}
        for step in range(2, last):
            batches[step] = (lanes * (2 * step - 1), lanes * (2 * step + 1))
        batches[last] = (lanes * (2 * last - 1), blocks)
    else:
        batches = {last: (0, blocks)}
    most = max(stop - first for first, stop in batches.values()) * rows
    dma, half = pltpu.SemaphoreType.DMA, jnp.bfloat16
    scratch = [pltpu.VMEM((blocks,) + a.shape, a.dtype) for a in arrays]
    scratch += [pltpu.VMEM(w.shape, w.dtype) for w in weights]
    scratch += [
        pltpu.VMEM((most, width), half),
        pltpu.VMEM((most, hidden), half),
        pltpu.VMEM((blocks, rows, width), half),
        pltpu.VMEM((2, last, 2, rows, width // 2), half),
        pltpu.VMEM((2, last, 2, rows, width // 2), half),
    ]
    need = sum(2 * (-(-rows // 16) * 16) * width * k for k in (2 * blocks, 4 * last, n))
    need += sum(w.size * 2 for w in weights) + 2 * most * (width + hidden) + 2**23
    if need > 58 * 2**20:
        return None
    scratch += [dma((2, last, count)), dma((2, last, count)), dma((2, last, 2)), dma((2, last, 2))]
    scratch += [dma((3,)), dma((count,))]
    if lanes == 2:
        scratch += [pltpu.VMEM((n, rows, width), half)]
        scratch += [dma((2 * last + 1, count)), dma((2 * last + 1, count)), dma((n,)), dma((n,))]
    memory = [pltpu.VMEM] * len(arrays) + [pl.ANY] * 3
    return pl.pallas_call(
        functools.partial(fused_kernel, loop, len(arrays) == 2, pieces, batches),
        out_shape=jax.ShapeDtypeStruct((rows, width), jnp.float32),
        in_specs=[pl.BlockSpec(memory_space=space) for space in memory],
        out_specs=pl.BlockSpec(memory_space=pltpu.VMEM),
        scratch_shapes=scratch,
        compiler_params=pltpu.CompilerParams(
            collective_id=collective_id, has_side_effects=True, vmem_limit_bytes=60 * 2**20
        ),
    )(*arrays, *weights)


def local(
    loop,
    hidden_rows,
    expert_ids,
    accepted,
    norm_gain,
    router,
    gate_weight,
    up_weight,
    down_weight,
    draft_gain,
    draft_gate,
    draft_up,
    draft_down,
    final_gain,
):
    rounds_total, rows_here, width = hidden_rows.shape
    expert_count = router.shape[1]
    requests_here = accepted.shape[1]
    draft_rows = rows_here // requests_here
    total = rounds_total * rows_here
    my_expert = lax.axis_index(RING)

    rows = hidden_rows.reshape(total, width).astype(jnp.float32)
    normed = rms_scale(rows, norm_gain).astype(jnp.bfloat16)
    logits = jnp.dot(normed, router, preferred_element_type=jnp.float32)
    ids = expert_ids.reshape(total, -1)
    named = jnp.any(ids[:, :, None] == jnp.arange(expert_count, dtype=jnp.int32), axis=1)
    weights = jnp.where(named, jnp.exp(logits), 0.0)
    table = weights / jnp.sum(weights, axis=1, keepdims=True)

    lanes_wide = -(-expert_count // 128) * 128
    table = jnp.pad(table, ((0, 0), (0, lanes_wide - expert_count)))
    mixed = fused(
        loop, 0, True, (normed, table), (gate_weight[0], up_weight[0], down_weight[0])
    )
    if mixed is None:
        everyone, tables = gather(loop, 0, normed, table)
        everyone = everyone.reshape(-1, width)
        share = jnp.sum(
            jnp.where(jnp.arange(lanes_wide) == my_expert, tables.reshape(-1, lanes_wide), 0.0),
            axis=1,
            keepdims=True,
        )
        gate_values = jnp.dot(everyone, gate_weight[0], preferred_element_type=jnp.float32)
        up_values = jnp.dot(everyone, up_weight[0], preferred_element_type=jnp.float32)
        active = (jax.nn.silu(gate_values) * up_values).astype(jnp.bfloat16)
        part = jnp.dot(active, down_weight[0], preferred_element_type=jnp.float32)
        part = (share * part).astype(jnp.bfloat16)
        mixed = scatter(loop, 1, part.reshape(-1, total, width))
    mixed = lax.psum(mixed, "sub")
    verified = (rows + mixed).astype(jnp.bfloat16)

    by_request = verified.reshape(rounds_total, requests_here, draft_rows, width)
    pick = jnp.arange(draft_rows, dtype=jnp.int32) == accepted[:, :, None]
    features = jnp.sum(jnp.where(pick[..., None], by_request.astype(jnp.float32), 0.0), axis=2)
    features = features.reshape(rounds_total * requests_here, width)
    draft_input = rms_scale(features, draft_gain).astype(jnp.bfloat16)
    summed = fused(loop, 2, False, (draft_input,), (draft_gate, draft_up, draft_down))
    if summed is None:
        (pieces,) = gather(loop, 2, draft_input)
        pieces = pieces.reshape(-1, width)
        gate_part = jnp.dot(pieces, draft_gate, preferred_element_type=jnp.float32)
        up_part = jnp.dot(pieces, draft_up, preferred_element_type=jnp.float32)
        units = (jax.nn.silu(gate_part) * up_part).astype(jnp.bfloat16)
        drafted = jnp.dot(units, draft_down, preferred_element_type=jnp.float32).astype(jnp.bfloat16)
        summed = scatter(loop, 3, drafted.reshape(-1, rounds_total * requests_here, width))
    draft_out = rms_scale(features + summed, final_gain).astype(jnp.bfloat16)
    return (
        verified.reshape(hidden_rows.shape),
        draft_out.reshape(rounds_total, requests_here, width),
    )


def solution(mesh):
    placed = (
        P(None, ("groups", "expert", "tensor"), None),
        P(None, ("groups", "expert", "tensor"), None),
        P(None, ("groups", "expert", "tensor")),
        P(),
        P(),
        P(("expert", "tensor"), None, "sub"),
        P(("expert", "tensor"), None, "sub"),
        P(("expert", "tensor"), "sub", None),
        P(),
        P(None, ("expert", "tensor")),
        P(None, ("expert", "tensor")),
        P(("expert", "tensor"), None),
        P(),
    )
    loop = Loop(dict(mesh.shape))
    return jax.shard_map(
        functools.partial(local, loop),
        mesh=mesh,
        in_specs=placed,
        out_specs=(
            P(None, ("groups", "expert", "tensor"), None),
            P(None, ("groups", "expert", "tensor"), None),
        ),
        check_vma=False,
    )
```
